32 devices in a mesh: fsdp: 2 (over y), replica: 16 (over z, x, core).
Axes of the slice: x: 2, y: 2, z: 4, core: 2. Of those that a mesh axis runs over, the one named last changes fastest.
Arguments:
- params: bfloat16 [16, 2, 2048, 512], P('replica', None, 'fsdp'), may hold values from -2.390625 to 2.390625
- momentum: bfloat16 [16, 2, 2048, 512], P('replica', None, 'fsdp'), may hold values from -6 to 6
- grads: bfloat16 [2, 16, 2, 2048, 512], P(None, 'replica', None, 'fsdp'), may hold values from -6 to 6
Outputs:
- new_params: bfloat16 [16, 2, 2048, 512], P('replica', None, 'fsdp')
- new_momentum: bfloat16 [16, 2, 2048, 512], P('replica', None, 'fsdp')
The draws below stay inside these ranges and needn't reach their ends.
All inputs are finite; a program needn't handle non-finite values.
Results may differ from the reference program's by a relative error of at most 0.013.
Values may be sent and summed in bfloat16 or wider, within the bound.
A program may use at most 128 MiB of HBM per device.

```python
import math
import jax
import jax.numpy as jnp
from jax import lax

ROWS = 2048
COLS = 512
NS_ITERS = 3
STEPS = 2
MATRICES = 2
REPLICAS = 16


def shard_levels(own_key, dims, shards, low, high):
    def one(position, blocks):
        draws = jax.random.uniform(jax.random.fold_in(jax.random.fold_in(own_key, 6), position), (blocks,), jnp.float32, low / len(shards), high / len(shards))
        return jnp.repeat(jnp.exp(draws), dims[position] // blocks).reshape((-1,) + (1,) * (len(dims) - position - 1))

    gain = one(*shards[0])
    for cut in shards[1:]:
        gain = gain * one(*cut)
    return gain


def normal_values(own_key, dims, width, limit, cuts=(), dtype=jnp.bfloat16):
    loudness = shard_levels(own_key, dims, cuts, -0.22, 0.18) if cuts else 1.0
    drawn = jax.random.normal(own_key, dims, jnp.float32) * width * loudness
    return jnp.minimum(jnp.maximum(drawn, -limit), limit).astype(dtype)


def setup_inputs(seed: int = 0) -> dict:
    splits = jax.random.split(jax.random.key(seed), 4)
    return {
        "params": normal_values(splits[0], (REPLICAS, MATRICES, ROWS, COLS), 0.3, 2.390625, ((0, 16), (2, 2))),
        "momentum": normal_values(splits[1], (REPLICAS, MATRICES, ROWS, COLS), 1.0, 6.0, ((0, 16), (2, 2))),
        "grads": normal_values(splits[2], (STEPS, REPLICAS, MATRICES, ROWS, COLS), 1.0, 6.0, ((1, 16), (3, 2))),
    }


BETA = 0.95
LEARN = 0.5
COEF_A = 3.4445
COEF_B = -4.775
COEF_C = 2.0315

def newton_schulz(matrix):
    xf = matrix.astype(jnp.float32)
    total = jnp.sqrt(jnp.sum(xf * xf))
    ycur = (xf / (total + 1e-07)).astype(jnp.bfloat16)
    for _ in range(NS_ITERS):
        gram = lax.dot_general(ycur, ycur, (((0,), (0,)), ((), ())), preferred_element_type=jnp.float32).astype(jnp.bfloat16)
        square = jnp.dot(gram, gram, preferred_element_type=jnp.float32)
        poly = (COEF_B * gram.astype(jnp.float32) + COEF_C * square).astype(jnp.bfloat16)
        ycur = (COEF_A * ycur.astype(jnp.float32) + jnp.dot(ycur, poly, preferred_element_type=jnp.float32)).astype(jnp.bfloat16)
    return ycur

def partner(values, span):
    shape = values.shape
    folded = values.reshape((shape[0] // (2 * span), 2, span) + shape[1:])
    return folded[:, ::-1].reshape(shape)

def reference(params, momentum, grads):
    step_scale = LEARN * 0.2 * math.sqrt(max(ROWS, COLS))
    pcur = params
    mcur = momentum
    for step in range(STEPS):
        grad = grads[step].astype(jnp.float32)
        m_new = (BETA * mcur.astype(jnp.float32) + grad).astype(jnp.bfloat16)
        nest = (grad + BETA * m_new.astype(jnp.float32)).astype(jnp.bfloat16)
        flat = nest.reshape(-1, ROWS, COLS)
        update = lax.map(newton_schulz, flat).reshape(nest.shape)
        local = (pcur.astype(jnp.float32) - step_scale * update.astype(jnp.float32)).astype(jnp.bfloat16)
        span = 2 ** step
        lfloat = local.astype(jnp.float32)
        pcur = (0.5 * (lfloat + partner(lfloat, span))).astype(jnp.bfloat16)
        mfloat = m_new.astype(jnp.float32)
        mcur = (0.5 * (mfloat + partner(mfloat, span))).astype(jnp.bfloat16)
    return (pcur, mcur)
```

```python
import math

import jax
import jax.numpy as jnp
from jax import lax
from jax.sharding import PartitionSpec as P

ROWS = 2048
COLS = 512
NS_ITERS = 3
STEPS = 2


BETA = 0.95
LEARN = 0.5
COEF_A = 3.4445
COEF_B = -4.775
COEF_C = 2.0315

BF16 = jnp.bfloat16
F32 = jnp.float32


def partner(value, axis, apart):
    mask = 2**apart
    pairs = [(source, source ^ mask) for source in range(lax.axis_size(axis))]
    return lax.ppermute(value, axis, pairs)


def dot(a, b):
    return jnp.dot(a, b, preferred_element_type=F32)


def reduce_gram(nest):
    part = lax.dot_general(nest, nest, (((0,), (0,)), ((), ())), preferred_element_type=F32)
    half = part.shape[0] // 2
    packed = jnp.concatenate([part[:half], part[half:, half:]], axis=1).astype(BF16)
    if lax.axis_size("fsdp") == 2:
        whole = packed.astype(F32) + partner(packed, "fsdp", 0).astype(F32)
    else:
        whole = lax.psum(packed.astype(F32), "fsdp")
    top, low = whole[:, : 2 * half], whole[:, 2 * half :]
    return jnp.concatenate([top, jnp.concatenate([top[:, half:].T, low], axis=1)], axis=0)


def orthogonalize(nest, gram):
    scale = 1.0 / (jnp.sqrt(jnp.trace(gram)) + 1e-07)
    gram = gram * (scale * scale)
    ycur = (nest.astype(F32) * scale).astype(BF16)
    for it in range(NS_ITERS):
        low = gram.astype(BF16)
        poly = (COEF_B * low.astype(F32) + COEF_C * dot(low, low)).astype(BF16)
        if it < NS_ITERS - 1:
            right = COEF_A * gram + dot(low, poly)
            gram = COEF_A * right + dot(poly, right.astype(BF16))
        ycur = COEF_A * ycur.astype(F32) + dot(ycur, poly)
        if it < NS_ITERS - 1:
            ycur = ycur.astype(BF16)
    return ycur


def mean(a, b):
    return (0.5 * (a.astype(F32) + b.astype(F32))).astype(BF16)


def shards(params, momentum, grads):
    mats = params.shape[1]
    step_scale = LEARN * 0.2 * math.sqrt(max(ROWS, COLS))
    nests = []
    mcur = [momentum[0, i] for i in range(mats)]
    for step in range(STEPS):
        grad = [grads[step, 0, i].astype(F32) for i in range(mats)]
        m_new = [(BETA * m.astype(F32) + g).astype(BF16) for m, g in zip(mcur, grad)]
        nests.append([(g + BETA * m.astype(F32)).astype(BF16) for m, g in zip(m_new, grad)])
        mcur = [mean(m, partner(m, "replica", step)) for m in m_new]
    grams = [[reduce_gram(n) for n in row] for row in nests]
    pcur = [params[0, i] for i in range(mats)]
    for step in range(STEPS):
        for i in range(mats):
            update = orthogonalize(nests[step][i], grams[step][i])
            local = (pcur[i].astype(F32) - step_scale * update).astype(BF16)
            pcur[i] = mean(local, partner(local, "replica", step))
    return (jnp.stack(pcur)[None], jnp.stack(mcur)[None])


def solution(mesh):
    return jax.shard_map(
        shards,
        mesh=mesh,
        in_specs=(
            P("replica", None, "fsdp", None),
            P("replica", None, "fsdp", None),
            P(None, "replica", None, "fsdp", None),
        ),
        out_specs=(P("replica", None, "fsdp", None), P("replica", None, "fsdp", None)),
        check_vma=False,
    )
```

```python
import functools
import math

import jax
import jax.numpy as jnp
from jax import lax
from jax.experimental import pallas as pl
from jax.experimental.pallas import tpu as pltpu
from jax.sharding import PartitionSpec as P

ROWS = 2048
COLS = 512
NS_ITERS = 3
STEPS = 2


BETA = 0.95
LEARN = 0.5
COEF_A = 3.4445
COEF_B = -4.775
COEF_C = 2.0315

MESH = pl.DeviceIdType.MESH
BF16 = jnp.bfloat16
F32 = jnp.float32


def partner(value, axis, apart):
    mask = 2**apart
    pairs = [(source, source ^ mask) for source in range(lax.axis_size(axis))]
    return lax.ppermute(value, axis, pairs)


def dot(a, b):
    return jnp.dot(a, b, preferred_element_type=F32)


def reduce_gram(nest):
    part = lax.dot_general(nest, nest, (((0,), (0,)), ((), ())), preferred_element_type=F32)
    half = part.shape[0] // 2
    packed = jnp.concatenate([part[:half], part[half:, half:]], axis=1).astype(BF16)
    if lax.axis_size("fsdp") == 2:
        whole = packed.astype(F32) + partner(packed, "fsdp", 0).astype(F32)
    else:
        whole = lax.psum(packed.astype(F32), "fsdp")
    top, low = whole[:, : 2 * half], whole[:, 2 * half :]
    return jnp.concatenate([top, jnp.concatenate([top[:, half:].T, low], axis=1)], axis=0)


def orthogonalize(nest, gram):
    scale = 1.0 / (jnp.sqrt(jnp.trace(gram)) + 1e-07)
    gram = gram * (scale * scale)
    ycur = (nest.astype(F32) * scale).astype(BF16)
    for it in range(NS_ITERS):
        low = gram.astype(BF16)
        poly = (COEF_B * low.astype(F32) + COEF_C * dot(low, low)).astype(BF16)
        if it < NS_ITERS - 1:
            right = COEF_A * gram + dot(low, poly)
            gram = COEF_A * right + dot(poly, right.astype(BF16))
        ycur = COEF_A * ycur.astype(F32) + dot(ycur, poly)
        if it < NS_ITERS - 1:
            ycur = ycur.astype(BF16)
    return ycur


def mean(a, b):
    return (0.5 * (a.astype(F32) + b.astype(F32))).astype(BF16)


def shards(params, momentum, grads):
    mats = params.shape[1]
    step_scale = LEARN * 0.2 * math.sqrt(max(ROWS, COLS))
    nests = []
    mcur = [momentum[0, i] for i in range(mats)]
    for step in range(STEPS):
        grad = [grads[step, 0, i].astype(F32) for i in range(mats)]
        m_new = [(BETA * m.astype(F32) + g).astype(BF16) for m, g in zip(mcur, grad)]
        nests.append([(g + BETA * m.astype(F32)).astype(BF16) for m, g in zip(m_new, grad)])
        mcur = [mean(m, partner(m, "replica", step)) for m in m_new]
    grams = [[reduce_gram(n) for n in row] for row in nests]
    pcur = [params[0, i] for i in range(mats)]
    for step in range(STEPS):
        for i in range(mats):
            update = orthogonalize(nests[step][i], grams[step][i])
            local = (pcur[i].astype(F32) - step_scale * update).astype(BF16)
            pcur[i] = mean(local, partner(local, "replica", step))
    return (jnp.stack(pcur)[None], jnp.stack(mcur)[None])


SUB = 64


def kernel(chunk, p_hbm, m_hbm, g_hbm, po_hbm, mo_hbm,
           p, m, g, mn1, rm1, mn2, rm2, n, l1, rl1, l2, rl2, gs, gr,
           gram, low, poly, right, rlow, isem, osem, ssem, rsem):
    mats, rows, cols = p.shape
    half = cols // 2
    per = rows // chunk
    count = mats * per
    step_scale = LEARN * 0.2 * math.sqrt(max(ROWS, COLS))
    side = lax.axis_index("fsdp")
    rep = lax.axis_index("replica")
    across = {"fsdp": 1 - side}
    near = {"replica": rep + 1 - 2 * (rep % 2)}
    far = {"replica": rep + 2 - 4 * ((rep // 2) % 2)}

    def span(index):
        return index // per, pl.ds(pl.multiple_of((index % per) * chunk, chunk), chunk)

    def sub(index, k):
        return index // per, pl.ds(pl.multiple_of((index % per) * chunk + k * SUB, SUB), SUB)

    loads = [(m_hbm, m, 0, (0,)), (g_hbm, g, 1, (0, 0)), (g_hbm, g, 2, (1, 0)), (p_hbm, p, 3, (0,))]

    def fetch(which, index):
        ref, vm, sem, lead = loads[which]
        i, r = span(index)
        dst = vm.at[lead[0], i, r] if len(lead) == 2 else vm.at[i, r]
        return pltpu.make_async_copy(ref.at[lead + (i, r)], dst, isem.at[sem * count + index])

    for index in range(count):
        for which in range(3):
            fetch(which, index).start()
    for index in range(count):
        fetch(3, index).start()

    barrier = pltpu.get_barrier_semaphore()
    for peer in (near, far, across):
        pl.semaphore_signal(barrier, inc=1, device_id=peer, device_id_type=MESH)
    pl.semaphore_wait(barrier, 3)

    def remote(src, dst, kind, index, peer):
        i, r = span(index)
        at = kind * count + index
        return pltpu.make_async_remote_copy(
            src_ref=src.at[i, r], dst_ref=dst.at[i, r], send_sem=ssem.at[at], recv_sem=rsem.at[at],
            device_id=peer, device_id_type=MESH)

    def first(index):
        return remote(mn1, rm1, 0, index, near)

    def second(index):
        return remote(mn2, rm2, 1, index, far)

    def third(index):
        return remote(l1, rl1, 2, index, near)

    def fourth(index):
        return remote(l2, rl2, 3, index, far)

    def blocks(step, i):
        at = 4 * count + step * mats + i
        return pltpu.make_async_remote_copy(
            src_ref=gs.at[step, i], dst_ref=gr.at[step, i], send_sem=ssem.at[at], recv_sem=rsem.at[at],
            device_id=across, device_id_type=MESH)

    def each(total, body):
        lax.fori_loop(0, total, lambda k, c: (body(k), c)[1], 0)

    def momentum_one(index):
        fetch(0, index).wait()
        fetch(1, index).wait()

        def body(k):
            i, r = sub(index, k)
            grad = g[0, i, r].astype(F32)
            new = (BETA * m[i, r].astype(F32) + grad).astype(BF16)
            mn1[i, r] = new
            n[0, i, r] = (grad + BETA * new.astype(F32)).astype(BF16)

        each(chunk // SUB, body)
        first(index).start()

    def momentum_two(index):
        fetch(2, index).wait()
        first(index).wait_recv()

        def body(k):
            i, r = sub(index, k)
            grad = g[1, i, r].astype(F32)
            cur = (0.5 * (mn1[i, r].astype(F32) + rm1[i, r].astype(F32))).astype(BF16)
            new = (BETA * cur.astype(F32) + grad).astype(BF16)
            mn2[i, r] = new
            n[1, i, r] = (grad + BETA * new.astype(F32)).astype(BF16)

        each(chunk // SUB, body)
        second(index).start()

    lag = min(LAG, count)
    for index in range(count + lag):
        if index < count:
            momentum_one(index)
        if index >= lag:
            momentum_two(index - lag)

    def gram_part(step, i):
        left, low_part = n[step, i, :, :half], n[step, i, :, half:]
        dims = (((0,), (0,)), ((), ()))
        gs[step, i, :, :cols] = lax.dot_general(left, n[step, i], dims, preferred_element_type=F32).astype(BF16)
        gs[step, i, :, cols:] = lax.dot_general(low_part, low_part, dims, preferred_element_type=F32).astype(BF16)
        blocks(step, i).start()

    each(STEPS * mats, lambda k: gram_part(k // mats, k % mats))

    def polys(step, i):
        blocks(step, i).wait_recv()
        top = gs[step, i, :, :cols].astype(F32) + gr[step, i, :, :cols].astype(F32)
        end = gs[step, i, :, cols:].astype(F32) + gr[step, i, :, cols:].astype(F32)
        eye = lax.broadcasted_iota(jnp.int32, (half, half), 0) == lax.broadcasted_iota(jnp.int32, (half, half), 1)
        trace = jnp.sum(jnp.where(eye, top[:, :half] + end, 0.0), keepdims=True)
        scale = 1.0 / (jnp.sqrt(trace) + 1e-07)
        square = scale * scale
        gram[:half, :] = top * square
        gram[half:, half:] = end * square
        gram[half:, :half] = (top[:, half:] * square).T
        low[...] = gram[...].astype(BF16)
        for it in range(NS_ITERS):
            def make_poly(t):
                r = pl.ds(pl.multiple_of(t * half, half), half)
                poly[it, r] = (COEF_B * low[r].astype(F32) + COEF_C * dot(low[r], low[...])).astype(BF16)

            def make_right(t):
                r = pl.ds(pl.multiple_of(t * half, half), half)
                value = COEF_A * gram[r] + dot(low[r], poly[it])
                right[r] = value
                rlow[r] = value.astype(BF16)

            def make_gram(t):
                r = pl.ds(pl.multiple_of(t * half, half), half)
                value = COEF_A * right[r] + dot(poly[it, r], rlow[...])
                gram[r] = value
                low[r] = value.astype(BF16)

            each(2, make_poly)
            if it < NS_ITERS - 1:
                each(2, make_right)
                each(2, make_gram)
        return scale

    def update(step, index, scale):
        i, r = span(index)
        ycur = (n[step, i, r].astype(F32) * scale).astype(BF16)
        for it in range(NS_ITERS):
            ycur = COEF_A * ycur.astype(F32) + dot(ycur, poly[it])
            if it < NS_ITERS - 1:
                ycur = ycur.astype(BF16)
        return ycur

    def step_one(i):
        scale = polys(0, i)

        def body(c):
            index = i * per + c
            i_, r = span(index)
            fetch(3, index).wait()
            l1[i_, r] = (p[i_, r].astype(F32) - step_scale * update(0, index, scale)).astype(BF16)
            third(index).start()

        each(per, body)

    def step_two(i):
        scale = polys(1, i)

        def body(c):
            index = i * per + c
            i_, r = span(index)
            third(index).wait_recv()
            cur = (0.5 * (l1[i_, r].astype(F32) + rl1[i_, r].astype(F32))).astype(BF16).astype(F32)
            l2[i_, r] = (cur - step_scale * update(1, index, scale)).astype(BF16)
            fourth(index).start()

        each(per, body)

    each(mats, step_one)
    each(mats, step_two)

    def store(ref, vm, kind, index):
        i, r = span(index)
        return pltpu.make_async_copy(vm.at[i, r], ref.at[0, i, r], osem.at[kind * count + index])

    def finish(ref, out, own, got, copy, kind, index):
        copy(index).wait_recv()

        def body(k):
            i, r = sub(index, k)
            out[i, r] = (0.5 * (own[i, r].astype(F32) + got[i, r].astype(F32))).astype(BF16)

        each(chunk // SUB, body)
        store(ref, out, kind, index).start()

    each(count, lambda index: finish(mo_hbm, m, mn2, rm2, second, 0, index))
    each(count, lambda index: finish(po_hbm, p, l2, rl2, fourth, 1, index))

    def drain(index):
        for copy in (first, second, third, fourth):
            copy(index).wait_send()
        store(mo_hbm, m, 0, index).wait()
        store(po_hbm, p, 1, index).wait()

    each(count, drain)
    each(STEPS * mats, lambda k: blocks(k // mats, k % mats).wait_send())


LAG = 2
CHUNK = 256


def fused(params, momentum, grads):
    _, mats, rows, cols = params.shape
    chunk = min(CHUNK, rows)
    count = mats * (rows // chunk)
    whole = pltpu.VMEM((mats, rows, cols), BF16)
    both = pltpu.VMEM((STEPS, mats, rows, cols), BF16)
    pack = pltpu.VMEM((STEPS, mats, cols // 2, cols + cols // 2), BF16)
    small, small_low = pltpu.VMEM((cols, cols), F32), pltpu.VMEM((cols, cols), BF16)
    dma = pltpu.SemaphoreType.DMA
    copies = 4 * count + STEPS * mats
    anywhere = pl.BlockSpec(memory_space=pl.ANY)
    return pl.pallas_call(
        functools.partial(kernel, chunk),
        out_shape=[jax.ShapeDtypeStruct(params.shape, BF16)] * 2,
        in_specs=[anywhere] * 3,
        out_specs=[anywhere] * 2,
        scratch_shapes=[
            whole, whole, both, whole, whole, whole, whole, both, whole, whole, whole, whole, pack, pack,
            small, small_low, pltpu.VMEM((NS_ITERS, cols, cols), BF16), small, small_low,
            dma((4 * count,)), dma((2 * count,)), dma((copies,)), dma((copies,)),
        ],
        compiler_params=pltpu.CompilerParams(
            collective_id=0, has_side_effects=True, vmem_limit_bytes=60 * 2**20),
    )(params, momentum, grads)


def solution(mesh):
    return jax.shard_map(
        fused if mesh.shape["fsdp"] == 2 else shards,
        mesh=mesh,
        in_specs=(
            P("replica", None, "fsdp", None),
            P("replica", None, "fsdp", None),
            P(None, "replica", None, "fsdp", None),
        ),
        out_specs=(P("replica", None, "fsdp", None), P("replica", None, "fsdp", None)),
        check_vma=False,
    )
```

```python
import functools
import math

import jax
import jax.numpy as jnp
from jax import lax
from jax.experimental import pallas as pl
from jax.experimental.pallas import tpu as pltpu
from jax.sharding import PartitionSpec as P

ROWS = 2048
COLS = 512
NS_ITERS = 3
STEPS = 2


BETA = 0.95
LEARN = 0.5
COEF_A = 3.4445
COEF_B = -4.775
COEF_C = 2.0315

MESH = pl.DeviceIdType.MESH
BF16 = jnp.bfloat16
F32 = jnp.float32


def partner(value, axis, apart):
    mask = 2**apart
    pairs = [(source, source ^ mask) for source in range(lax.axis_size(axis))]
    return lax.ppermute(value, axis, pairs)


def dot(a, b):
    return jnp.dot(a, b, preferred_element_type=F32)


def reduce_gram(nest):
    part = lax.dot_general(nest, nest, (((0,), (0,)), ((), ())), preferred_element_type=F32)
    half = part.shape[0] // 2
    packed = jnp.concatenate([part[:half], part[half:, half:]], axis=1).astype(BF16)
    if lax.axis_size("fsdp") == 2:
        whole = packed.astype(F32) + partner(packed, "fsdp", 0).astype(F32)
    else:
        whole = lax.psum(packed.astype(F32), "fsdp")
    top, low = whole[:, : 2 * half], whole[:, 2 * half :]
    return jnp.concatenate([top, jnp.concatenate([top[:, half:].T, low], axis=1)], axis=0)


def orthogonalize(nest, gram):
    scale = 1.0 / (jnp.sqrt(jnp.trace(gram)) + 1e-07)
    gram = gram * (scale * scale)
    ycur = (nest.astype(F32) * scale).astype(BF16)
    for it in range(NS_ITERS):
        low = gram.astype(BF16)
        poly = (COEF_B * low.astype(F32) + COEF_C * dot(low, low)).astype(BF16)
        if it < NS_ITERS - 1:
            right = COEF_A * gram + dot(low, poly)
            gram = COEF_A * right + dot(poly, right.astype(BF16))
        ycur = COEF_A * ycur.astype(F32) + dot(ycur, poly)
        if it < NS_ITERS - 1:
            ycur = ycur.astype(BF16)
    return ycur


def mean(a, b):
    return (0.5 * (a.astype(F32) + b.astype(F32))).astype(BF16)


def shards(params, momentum, grads):
    mats = params.shape[1]
    step_scale = LEARN * 0.2 * math.sqrt(max(ROWS, COLS))
    nests = []
    mcur = [momentum[0, i] for i in range(mats)]
    for step in range(STEPS):
        grad = [grads[step, 0, i].astype(F32) for i in range(mats)]
        m_new = [(BETA * m.astype(F32) + g).astype(BF16) for m, g in zip(mcur, grad)]
        nests.append([(g + BETA * m.astype(F32)).astype(BF16) for m, g in zip(m_new, grad)])
        mcur = [mean(m, partner(m, "replica", step)) for m in m_new]
    grams = [[reduce_gram(n) for n in row] for row in nests]
    pcur = [params[0, i] for i in range(mats)]
    for step in range(STEPS):
        for i in range(mats):
            update = orthogonalize(nests[step][i], grams[step][i])
            local = (pcur[i].astype(F32) - step_scale * update).astype(BF16)
            pcur[i] = mean(local, partner(local, "replica", step))
    return (jnp.stack(pcur)[None], jnp.stack(mcur)[None])


SUB = 64


def kernel(chunk, p_hbm, m_hbm, g_hbm, p_out, m_out,
           p, m, g, mn1, rm1, mn2, rm2, n, l1, rl1, l2, rl2, gs, gr,
           gram, low, poly, right, rlow, isem, ssem, rsem):
    mats, rows, cols = p.shape
    half = cols // 2
    per = rows // chunk
    count = mats * per
    step_scale = LEARN * 0.2 * math.sqrt(max(ROWS, COLS))
    side = lax.axis_index("fsdp")
    rep = lax.axis_index("replica")
    across = {"fsdp": 1 - side}
    near = {"replica": rep + 1 - 2 * (rep % 2)}
    far = {"replica": rep + 2 - 4 * ((rep // 2) % 2)}

    def span(index):
        return index // per, pl.ds(pl.multiple_of((index % per) * chunk, chunk), chunk)

    def sub(index, k):
        return index // per, pl.ds(pl.multiple_of((index % per) * chunk + k * SUB, SUB), SUB)

    loads = [(m_hbm, m, 0, (0,)), (g_hbm, g, 1, (0, 0)), (g_hbm, g, 2, (1, 0)), (p_hbm, p, 3, (0,))]

    def fetch(which, index):
        ref, vm, sem, lead = loads[which]
        i, r = span(index)
        dst = vm.at[lead[0], i, r] if len(lead) == 2 else vm.at[i, r]
        return pltpu.make_async_copy(ref.at[lead + (i, r)], dst, isem.at[sem * count + index])

    barrier = pltpu.get_barrier_semaphore()
    for peer in (near, far, across):
        pl.semaphore_signal(barrier, inc=1, device_id=peer, device_id_type=MESH)
    for index in range(count):
        for which in range(3):
            fetch(which, index).start()
    for index in range(count):
        fetch(3, index).start()

    def remote(src, dst, kind, index, peer):
        i, r = span(index)
        at = kind * count + index
        return pltpu.make_async_remote_copy(
            src_ref=src.at[i, r], dst_ref=dst.at[i, r], send_sem=ssem.at[at], recv_sem=rsem.at[at],
            device_id=peer, device_id_type=MESH)

    def first(index):
        return remote(mn1, rm1, 0, index, near)

    def second(index):
        return remote(mn2, rm2, 1, index, far)

    def third(index):
        return remote(l1, rl1, 2, index, near)

    def fourth(index):
        return remote(l2, rl2, 3, index, far)

    def blocks(step, i):
        at = 4 * count + step * mats + i
        return pltpu.make_async_remote_copy(
            src_ref=gs.at[step, i], dst_ref=gr.at[step, i], send_sem=ssem.at[at], recv_sem=rsem.at[at],
            device_id=across, device_id_type=MESH)

    def each(total, body):
        lax.fori_loop(0, total, lambda k, c: (body(k), c)[1], 0)

    def momentum_one(index):
        fetch(0, index).wait()
        fetch(1, index).wait()

        def body(k):
            i, r = sub(index, k)
            grad = g[0, i, r].astype(F32)
            new = (BETA * m[i, r].astype(F32) + grad).astype(BF16)
            mn1[i, r] = new
            n[0, i, r] = (grad + BETA * new.astype(F32)).astype(BF16)

        each(chunk // SUB, body)
        if index == 0:
            pl.semaphore_wait(barrier, 3)
        first(index).start()

    def momentum_two(index):
        fetch(2, index).wait()
        first(index).wait_recv()

        def body(k):
            i, r = sub(index, k)
            grad = g[1, i, r].astype(F32)
            cur = (0.5 * (mn1[i, r].astype(F32) + rm1[i, r].astype(F32))).astype(BF16)
            new = (BETA * cur.astype(F32) + grad).astype(BF16)
            mn2[i, r] = new
            n[1, i, r] = (grad + BETA * new.astype(F32)).astype(BF16)

        each(chunk // SUB, body)
        second(index).start()

    lag = min(LAG, count)
    for index in range(count + lag):
        if index < count:
            momentum_one(index)
        if index >= lag:
            momentum_two(index - lag)

    def gram_part(step, i):
        left, low_part = n[step, i, :, :half], n[step, i, :, half:]
        dims = (((0,), (0,)), ((), ()))
        gs[step, i, :, :cols] = lax.dot_general(left, n[step, i], dims, preferred_element_type=F32).astype(BF16)
        gs[step, i, :, cols:] = lax.dot_general(low_part, low_part, dims, preferred_element_type=F32).astype(BF16)
        blocks(step, i).start()

    each(STEPS * mats, lambda k: gram_part(k // mats, k % mats))

    def polys(step, i):
        blocks(step, i).wait_recv()
        top = gs[step, i, :, :cols].astype(F32) + gr[step, i, :, :cols].astype(F32)
        end = gs[step, i, :, cols:].astype(F32) + gr[step, i, :, cols:].astype(F32)
        eye = lax.broadcasted_iota(jnp.int32, (half, half), 0) == lax.broadcasted_iota(jnp.int32, (half, half), 1)
        trace = jnp.sum(jnp.where(eye, top[:, :half] + end, 0.0), keepdims=True)
        scale = 1.0 / (jnp.sqrt(trace) + 1e-07)
        square = scale * scale
        gram[:half, :] = top * square
        gram[half:, half:] = end * square
        gram[half:, :half] = (top[:, half:] * square).T
        low[...] = gram[...].astype(BF16)
        for it in range(NS_ITERS):
            def make_poly(t):
                r = pl.ds(pl.multiple_of(t * half, half), half)
                poly[it, r] = (COEF_B * low[r].astype(F32) + COEF_C * dot(low[r], low[...])).astype(BF16)

            def make_right(t):
                r = pl.ds(pl.multiple_of(t * half, half), half)
                value = COEF_A * gram[r] + dot(low[r], poly[it])
                right[r] = value
                rlow[r] = value.astype(BF16)

            def make_gram(t):
                r = pl.ds(pl.multiple_of(t * half, half), half)
                value = COEF_A * right[r] + dot(poly[it, r], rlow[...])
                gram[r] = value
                low[r] = value.astype(BF16)

            each(2, make_poly)
            if it < NS_ITERS - 1:
                each(2, make_right)
                each(2, make_gram)
        return scale

    def update(step, index, scale):
        i, r = span(index)
        ycur = (n[step, i, r].astype(F32) * scale).astype(BF16)
        for it in range(NS_ITERS):
            ycur = COEF_A * ycur.astype(F32) + dot(ycur, poly[it])
            if it < NS_ITERS - 1:
                ycur = ycur.astype(BF16)
        return ycur

    def step_one(i):
        scale = polys(0, i)

        def body(c):
            index = i * per + c
            i_, r = span(index)
            fetch(3, index).wait()
            l1[i_, r] = (p[i_, r].astype(F32) - step_scale * update(0, index, scale)).astype(BF16)
            third(index).start()

        each(per, body)

    def step_two(i):
        scale = polys(1, i)

        def body(c):
            index = i * per + c
            i_, r = span(index)
            third(index).wait_recv()
            cur = (0.5 * (l1[i_, r].astype(F32) + rl1[i_, r].astype(F32))).astype(BF16).astype(F32)
            l2[i_, r] = (cur - step_scale * update(1, index, scale)).astype(BF16)
            fourth(index).start()

        each(per, body)

    each(mats, step_one)
    each(mats, step_two)

    def finish(out, own, got, copy, index):
        copy(index).wait_recv()

        def body(k):
            i, r = sub(index, k)
            out[0, i, r] = (0.5 * (own[i, r].astype(F32) + got[i, r].astype(F32))).astype(BF16)

        each(chunk // SUB, body)

    each(count, lambda index: finish(m_out, mn2, rm2, second, index))
    each(count, lambda index: finish(p_out, l2, rl2, fourth, index))

    def drain(index):
        for copy in (first, second, third, fourth):
            copy(index).wait_send()

    each(count, drain)
    each(STEPS * mats, lambda k: blocks(k // mats, k % mats).wait_send())


def put(p, m, p_out, m_out, sem):
    copies = [
        pltpu.make_async_copy(src.at[0, i], dst.at[0, i], sem.at[k, i])
        for k, (src, dst) in enumerate(((p, p_out), (m, m_out))) for i in range(p.shape[1])
    ]
    for copy in copies:
        copy.start()
    for copy in copies:
        copy.wait()


LAG = 2
CHUNK = 256


def fused(params, momentum, grads):
    _, mats, rows, cols = params.shape
    chunk = min(CHUNK, rows)
    count = mats * (rows // chunk)
    whole = pltpu.VMEM((mats, rows, cols), BF16)
    both = pltpu.VMEM((STEPS, mats, rows, cols), BF16)
    pack = pltpu.VMEM((STEPS, mats, cols // 2, cols + cols // 2), BF16)
    small, small_low = pltpu.VMEM((cols, cols), F32), pltpu.VMEM((cols, cols), BF16)
    dma = pltpu.SemaphoreType.DMA
    copies = 4 * count + STEPS * mats
    anywhere = pl.BlockSpec(memory_space=pl.ANY)
    results = pl.pallas_call(
        functools.partial(kernel, chunk),
        out_shape=[pltpu.VMEM(params.shape, BF16)] * 2,
        in_specs=[anywhere] * 3,
        out_specs=[pl.BlockSpec(memory_space=pltpu.VMEM)] * 2,
        scratch_shapes=[
            whole, whole, both, whole, whole, whole, whole, both, whole, whole, whole, whole, pack, pack,
            small, small_low, pltpu.VMEM((NS_ITERS, cols, cols), BF16), small, small_low,
            dma((4 * count,)), dma((copies,)), dma((copies,)),
        ],
        compiler_params=pltpu.CompilerParams(
            collective_id=0, has_side_effects=True, vmem_limit_bytes=59 * 2**20),
    )(params, momentum, grads)
    return pl.pallas_call(
        put,
        out_shape=[jax.ShapeDtypeStruct(params.shape, BF16)] * 2,
        in_specs=[pl.BlockSpec(memory_space=pltpu.VMEM)] * 2,
        out_specs=[anywhere] * 2,
        scratch_shapes=[dma((2, mats))],
        compiler_params=pltpu.CompilerParams(vmem_limit_bytes=2**20),
    )(*[pltpu.with_memory_space_constraint(r, pltpu.VMEM) for r in results])


def solution(mesh):
    return jax.shard_map(
        fused if mesh.shape["fsdp"] == 2 else shards,
        mesh=mesh,
        in_specs=(
            P("replica", None, "fsdp", None),
            P("replica", None, "fsdp", None),
            P(None, "replica", None, "fsdp", None),
        ),
        out_specs=(P("replica", None, "fsdp", None), P("replica", None, "fsdp", None)),
        check_vma=False,
    )
```
